32 devices in a mesh: ens: 2 (over y), grid: 16 (over z, x, core).
Axes of the slice: x: 2, y: 2, z: 4, core: 2. Of those that a mesh axis runs over, the one named last changes fastest.
Arguments:
- fields: bfloat16 [2, 384, 768, 256], P('ens', 'grid'), may hold values from -6 to 6
- mode_counts: int32 [384], P('grid'), may hold values from 96 to 384, as said below
- gain_attn: float32 [256], replicated, may hold values from 0.5 to 1.5
- w_query: bfloat16 [256, 256], replicated, may hold values from -1 to 1
- w_key: bfloat16 [256, 256], replicated, may hold values from -8 to 8
- w_value: bfloat16 [256, 256], replicated, may hold values from -0.375 to 0.375
- w_out: bfloat16 [256, 256], replicated, may hold values from -0.375 to 0.375
- gain_spec: float32 [256], replicated, may hold values from 0.5 to 1.5
- w_first: bfloat16 [2, 8, 32, 32], replicated, may hold values from -1 to 1
- w_second: bfloat16 [2, 8, 32, 32], replicated, may hold values from -1 to 1
Outputs:
- layer_out: bfloat16 [2, 384, 768, 256], P('ens', 'grid')
The draws below stay inside these ranges and needn't reach their ends.
Inputs may be any that keep to these rules, and one draw needn't show every extreme that they name: `mode_counts`: longitude wavenumbers kept in each latitude row; some row keeps all 384.
All inputs are finite; a program needn't handle non-finite values.
Results may differ from the reference program's by a relative error of at most 0.012.
Values may be sent and summed in bfloat16 or wider, within the bound.
A program may use at most 256 MiB of HBM per device.

```python
import math
import jax
import jax.numpy as jnp
from jax import lax

D = 256
HEAD = 32
HEADS = 8
BLOCK = 32
NBLK = 8
NLAT = 384
NLON = 768
KLON = 384
KLAT = 128
MEMBERS = 2


def draw_pair(key):
    shared_part = jax.random.normal(jax.random.fold_in(key, 11), (D, D), jnp.float32) / math.sqrt(D)
    own_part = jax.random.normal(jax.random.fold_in(key, 12), (D, D), jnp.float32) / math.sqrt(D)
    return (shared_part, own_part)


def draw_w_query(key, part):
    shared_part, own_part = draw_pair(key)
    return jnp.clip(shared_part, -1.0, 1.0).astype(jnp.bfloat16)


def draw_w_key(key, part):
    shared_part, own_part = draw_pair(key)
    return jnp.clip(own_part, -8.0, 8.0).astype(jnp.bfloat16)


def draw_mode_counts(key, part):
    counts = jax.random.randint(jax.random.fold_in(key, 21), (NLAT,), KLON // 4, KLON + 1)
    chosen = jax.random.randint(jax.random.fold_in(key, 22), (), 0, NLAT)
    return jnp.where(jnp.arange(NLAT, dtype=jnp.int32) == chosen, KLON, counts).astype(jnp.int32)


def block_scale(rng, shape, cuts, smallest, largest):
    gain, own = 1.0, jax.random.fold_in(rng, 6)
    for axis_at, parts in cuts:
        draws = jnp.exp(jax.random.uniform(jax.random.fold_in(own, axis_at), (parts,), jnp.float32, smallest / len(cuts), largest / len(cuts)))
        gain = gain * jnp.repeat(draws, shape[axis_at] // parts).reshape([-1 if axis == axis_at else 1 for axis in range(len(shape))])
    return gain


def noise(stream_key, extent, width, most, cuts=(), held_as=jnp.bfloat16):
    gain = block_scale(stream_key, extent, cuts, -0.22, 0.18) if cuts else 1.0
    result = jax.random.normal(stream_key, extent, jnp.float32) * width * gain
    return jnp.minimum(jnp.maximum(result, -most), most).astype(held_as)


def setup_inputs(seed: int = 0) -> dict:
    arg_keys = jax.random.split(jax.random.key(seed), 11)
    return {
        "fields": noise(arg_keys[0], (MEMBERS, NLAT, NLON, D), 1.0, 6.0, ((0, 2), (1, 16))),
        "mode_counts": draw_mode_counts(jax.random.fold_in(arg_keys[10], 71), 0),
        "gain_attn": jnp.clip(1.0 + 0.1 * jax.random.normal(arg_keys[2], (D,), jnp.float32), 0.5, 1.5),
        "w_query": draw_w_query(jax.random.fold_in(arg_keys[10], 71), 0),
        "w_key": draw_w_key(jax.random.fold_in(arg_keys[10], 71), 0),
        "w_value": noise(arg_keys[5], (D, D), D ** -0.5, 0.375),
        "w_out": noise(arg_keys[6], (D, D), D ** -0.5, 0.375),
        "gain_spec": jnp.clip(1.0 + 0.1 * jax.random.normal(arg_keys[7], (D,), jnp.float32), 0.5, 1.5),
        "w_first": noise(arg_keys[8], (2, NBLK, BLOCK, BLOCK), BLOCK ** -0.5, 1.0),
        "w_second": noise(arg_keys[9], (2, NBLK, BLOCK, BLOCK), BLOCK ** -0.5, 1.0),
    }


norm_eps = 1e-05

def layer_norm(inputs, gain_vec):
    widened = inputs.astype(jnp.float32)
    center = widened - lax.optimization_barrier(jnp.mean(widened, axis=-1, keepdims=True))
    spread = lax.optimization_barrier(jnp.mean(center * center, axis=-1, keepdims=True))
    return center * lax.rsqrt(spread + norm_eps) * gain_vec

def lon_table(points, mode_count):
    positions = jnp.arange(points, dtype=jnp.int32)
    frequency = jnp.arange(mode_count, dtype=jnp.int32)
    turn_count = positions[:, None] * frequency[None, :] % points
    angles = 2.0 * math.pi / points * turn_count.astype(jnp.float32)
    factor = 1.0 / math.sqrt(points)
    return jnp.concatenate([jnp.cos(angles) * factor, -jnp.sin(angles) * factor], axis=1).astype(jnp.bfloat16)

def lon_inverse(points, mode_count):
    positions = jnp.arange(points, dtype=jnp.int32)
    frequency = jnp.arange(mode_count, dtype=jnp.int32)
    turn_count = frequency[:, None] * positions[None, :] % points
    angles = 2.0 * math.pi / points * turn_count.astype(jnp.float32)
    weight = jnp.where(frequency == 0, 1.0, 2.0).astype(jnp.float32)[:, None] / math.sqrt(points)
    return jnp.stack([jnp.cos(angles) * weight, -jnp.sin(angles) * weight]).astype(jnp.bfloat16)

def lat_angles(row_count, mode_count):
    frequency = jnp.arange(mode_count, dtype=jnp.int32)
    frequency = jnp.where(frequency < mode_count // 2, frequency, frequency - mode_count)
    positions = jnp.arange(row_count, dtype=jnp.int32)
    turn_count = frequency[:, None] * positions[None, :] % row_count
    return 2.0 * math.pi / row_count * turn_count.astype(jnp.float32)

def lat_forward(row_count, mode_count):
    angles = lat_angles(row_count, mode_count)
    factor = 1.0 / math.sqrt(row_count)
    cosine = jnp.cos(angles) * factor
    sine_part = jnp.sin(angles) * factor
    return jnp.stack([jnp.stack([cosine, sine_part], axis=1), jnp.stack([-sine_part, cosine], axis=1)]).astype(jnp.bfloat16)

def lat_inverse(row_count, mode_count):
    angles = jnp.transpose(lat_angles(row_count, mode_count))
    factor = 1.0 / math.sqrt(row_count)
    cosine = jnp.cos(angles) * factor
    sine_part = jnp.sin(angles) * factor
    return jnp.stack([jnp.stack([cosine, -sine_part]), jnp.stack([sine_part, cosine])]).astype(jnp.bfloat16)

def complex_blocks(weight):
    real_part = weight[0]
    imag_part = weight[1]
    return jnp.stack([jnp.stack([real_part, imag_part]), jnp.stack([-imag_part, real_part])])

def mix_blocks(spec, big):
    blocks = spec.reshape(spec.shape[:3] + (big.shape[2], big.shape[3]))
    out_blocks = jnp.einsum('pqkbi,psbio->sqkbo', blocks.astype(jnp.float32), big.astype(jnp.float32))
    return out_blocks.reshape(spec.shape)

def reference(fields, mode_counts, gain_attn, w_query, w_key, w_value, w_out, gain_spec, w_first, w_second):
    score_scale = 1.0 / math.sqrt(HEAD)

    def attend(lat_row):
        normed = layer_norm(lat_row, gain_attn).astype(jnp.bfloat16)
        queries = jnp.dot(normed, w_query, preferred_element_type=jnp.float32).astype(jnp.bfloat16)
        key_rows = jnp.dot(normed, w_key, preferred_element_type=jnp.float32).astype(jnp.bfloat16)
        value_rows = jnp.dot(normed, w_value, preferred_element_type=jnp.float32).astype(jnp.bfloat16)
        queries = queries.reshape(MEMBERS, NLON, HEADS, HEAD).astype(jnp.float32)
        key_rows = key_rows.reshape(MEMBERS, NLON, HEADS, HEAD).astype(jnp.float32)
        value_rows = value_rows.reshape(MEMBERS, NLON, HEADS, HEAD).astype(jnp.float32)
        scores = jnp.einsum('mwhe,nwhe->nmhw', queries, key_rows) * score_scale
        row_max = lax.optimization_barrier(jnp.max(scores, axis=0, keepdims=True))
        exps = jnp.exp(scores - row_max)
        totals = lax.optimization_barrier(jnp.sum(exps, axis=0))
        weights = exps.astype(jnp.bfloat16).astype(jnp.float32)
        mixed_out = jnp.einsum('nmhw,nwhe->mwhe', weights, value_rows)
        mixed_out = mixed_out / jnp.transpose(totals, (0, 2, 1))[..., None]
        mixed_out = mixed_out.astype(jnp.bfloat16).reshape(MEMBERS, NLON, D)
        return (lat_row.astype(jnp.float32) + jnp.dot(mixed_out, w_out, preferred_element_type=jnp.float32)).astype(jnp.bfloat16)
    attended = jnp.moveaxis(lax.map(attend, jnp.moveaxis(fields, 1, 0)), 0, 1)
    retained = (jnp.arange(KLON, dtype=jnp.int32)[None, :] < mode_counts[:, None]).astype(jnp.float32)
    lon_fwd = lon_table(NLON, KLON).astype(jnp.float32)
    lon_back = lon_inverse(NLON, KLON).astype(jnp.float32)
    forward = lat_forward(NLAT, KLAT).astype(jnp.float32)
    inverse = lat_inverse(NLAT, KLAT).astype(jnp.float32)
    big_one = complex_blocks(w_first)
    big_two = complex_blocks(w_second)

    def spectral(member):
        normed_two = layer_norm(member, gain_spec).astype(jnp.bfloat16)
        spectrum = jnp.einsum('jxd,xk->jkd', normed_two.astype(jnp.float32), lon_fwd)
        spectrum = (spectrum.reshape(NLAT, 2, KLON, D) * retained[:, None, :, None]).astype(jnp.bfloat16)
        rows_spec = jnp.einsum('pqrj,jrkd->pqkd', forward, spectrum.astype(jnp.float32)).astype(jnp.bfloat16)
        hidden = jnp.maximum(mix_blocks(rows_spec, big_one), 0.0).astype(jnp.bfloat16)
        second = mix_blocks(hidden, big_two).astype(jnp.bfloat16)
        back_rows = jnp.einsum('rpjq,pqkd->jrkd', inverse, second.astype(jnp.float32))
        back_rows = (back_rows * retained[:, None, :, None]).astype(jnp.bfloat16)
        field_out = jnp.einsum('jrkd,rkx->jxd', back_rows.astype(jnp.float32), lon_back)
        return (member.astype(jnp.float32) + field_out).astype(jnp.bfloat16)
    return lax.map(spectral, attended)
```

```python
import functools
import math

import jax
import jax.numpy as jnp
from jax import lax
from jax.experimental import pallas as pl
from jax.experimental.pallas import tpu as pltpu
from jax.sharding import PartitionSpec as P

HEAD = 32
NLAT = 384
KLON = 384
KLAT = 128
CHUNKS = 4

norm_eps = 1e-05


def layer_norm(widened, gain_vec):
    center = widened - jnp.mean(widened, axis=-1, keepdims=True)
    spread = jnp.mean(center * center, axis=-1, keepdims=True)
    return (center * lax.rsqrt(spread + norm_eps) * gain_vec).astype(jnp.bfloat16)


def wave_order(groups):
    held = KLON // groups
    place = jnp.arange(2 * KLON, dtype=jnp.int32)
    part = place // held % 2
    wave = place // (2 * held) * held + place % held
    return part, wave


def lon_forward(points, groups):
    part, wave = wave_order(groups)
    positions = jnp.arange(points, dtype=jnp.int32)
    turn_count = wave[:, None] * positions[None, :] % points
    angles = 2.0 * math.pi / points * turn_count.astype(jnp.float32)
    factor = 1.0 / math.sqrt(points)
    return jnp.where(
        part[:, None] == 0, jnp.cos(angles) * factor, -jnp.sin(angles) * factor
    ).astype(jnp.bfloat16)


def lon_inverse(points, groups):
    part, wave = wave_order(groups)
    positions = jnp.arange(points, dtype=jnp.int32)
    turn_count = positions[:, None] * wave[None, :] % points
    angles = 2.0 * math.pi / points * turn_count.astype(jnp.float32)
    weight = jnp.where(wave == 0, 1.0, 2.0).astype(jnp.float32)[None, :] / math.sqrt(points)
    return jnp.where(
        part[None, :] == 0, jnp.cos(angles) * weight, -jnp.sin(angles) * weight
    ).astype(jnp.bfloat16)


def lat_angles(row_count, mode_count):
    frequency = jnp.arange(mode_count, dtype=jnp.int32)
    frequency = jnp.where(frequency < mode_count // 2, frequency, frequency - mode_count)
    positions = jnp.arange(row_count, dtype=jnp.int32)
    turn_count = frequency[:, None] * positions[None, :] % row_count
    return 2.0 * math.pi / row_count * turn_count.astype(jnp.float32)


def lat_forward(row_count, mode_count):
    angles = lat_angles(row_count, mode_count)
    factor = 1.0 / math.sqrt(row_count)
    cosine = jnp.cos(angles) * factor
    sine_part = jnp.sin(angles) * factor
    return jnp.stack(
        [jnp.stack([cosine, sine_part], axis=1), jnp.stack([-sine_part, cosine], axis=1)]
    ).astype(jnp.bfloat16)


def lat_inverse(row_count, mode_count):
    angles = jnp.transpose(lat_angles(row_count, mode_count))
    factor = 1.0 / math.sqrt(row_count)
    cosine = jnp.cos(angles) * factor
    sine_part = jnp.sin(angles) * factor
    return jnp.stack([jnp.stack([cosine, -sine_part]), jnp.stack([sine_part, cosine])]).astype(
        jnp.bfloat16
    )


def complex_blocks(weight):
    real_part = weight[0]
    imag_part = weight[1]
    return jnp.stack([jnp.stack([real_part, imag_part]), jnp.stack([-imag_part, real_part])])


def mix_blocks(spec, big):
    blocks = spec.reshape(spec.shape[:3] + (big.shape[2], big.shape[3]))
    out_blocks = jnp.einsum("pqkbi,psbio->sqkbo", blocks, big, preferred_element_type=jnp.float32)
    return out_blocks.reshape(spec.shape)


def dot(left, right):
    return jnp.dot(left, right, preferred_element_type=jnp.float32)


def attend_kernel(others, first_row, sub, counts, own, *refs):
    other_refs = refs[:others]
    (gain_one, w_qkv, w_out, gain_two, table, sums, waves, attended, spectrum, normed) = refs[others:]
    points, feat = own.shape[1:]
    scale = 1.0 / math.sqrt(HEAD)
    for start in range(0, points, sub):
        rows = pl.ds(start, sub)
        fields = own[0, rows, :].astype(jnp.float32)
        joined = dot(layer_norm(fields, gain_one[...]), w_qkv[...]).astype(jnp.bfloat16)
        queries = joined[:, :feat].astype(jnp.float32)
        own_keys = joined[:, feat : 2 * feat].astype(jnp.float32)
        values = [joined[:, 2 * feat :].astype(jnp.float32)]
        shifted = [jnp.zeros((sub, feat), jnp.float32)]
        for ref in other_refs:
            side = layer_norm(ref[0, rows, :].astype(jnp.float32), gain_one[...])
            pair = dot(side, w_qkv[:, feat:]).astype(jnp.bfloat16)
            terms = queries * (pair[:, :feat].astype(jnp.float32) - own_keys)
            upper = terms.astype(jnp.bfloat16)
            lower = (terms - upper.astype(jnp.float32)).astype(jnp.bfloat16)
            total = dot(upper, sums[...]) + dot(lower, sums[...])
            shifted.append(total * scale)
            values.append(pair[:, feat:].astype(jnp.float32))
        largest = functools.reduce(jnp.maximum, shifted)
        exps = [jnp.exp(item - largest) for item in shifted]
        totals = functools.reduce(jnp.add, exps)
        mixed = functools.reduce(
            jnp.add,
            [e.astype(jnp.bfloat16).astype(jnp.float32) * v for e, v in zip(exps, values)],
        )
        mixed = (mixed / totals).astype(jnp.bfloat16)
        result = (fields + dot(mixed, w_out[...])).astype(jnp.bfloat16)
        attended[0, rows, :] = result
        normed[rows, :] = layer_norm(result.astype(jnp.float32), gain_two[...])
    kept = waves[...] < counts[first_row + pl.program_id(0)]
    spec = dot(table[...], normed[...])
    spec = jnp.where(kept, spec, 0.0).astype(jnp.bfloat16)
    if len(spectrum.shape) == 4:
        spectrum[:, 0] = spec.reshape(spectrum.shape[0], spectrum.shape[2], feat)
    else:
        spectrum[0] = spec


def attend(chunk, rows, aligned, groups, fields, others, counts, gains, weights, tables):
    points, feat = fields.shape[1:]
    first_row = chunk * rows
    sub = points // 3 if points % 48 == 0 else points
    whole = lambda a: pl.BlockSpec(a.shape, lambda i, c: (0,) * a.ndim)
    w_qkv, w_out = weights
    table, sums, waves = tables
    held = 2 * KLON // groups
    if aligned:
        spec_shape = (groups, rows, held, feat)
        spec_block = pl.BlockSpec((groups, 1, held, feat), lambda i, c: (0, i, 0, 0))
    else:
        spec_shape = (rows, 2 * KLON, feat)
        spec_block = pl.BlockSpec((1, 2 * KLON, feat), lambda i, c: (i, 0, 0))
    row_block = pl.BlockSpec((1, points, feat), lambda i, c: (i, 0, 0))
    own_block = pl.BlockSpec((1, points, feat), lambda i, c: (first_row + i, 0, 0))
    params = (gains[0], w_qkv, w_out, gains[1], table, sums, waves)
    flops = 2 * rows * points * feat * (feat * 8 + 2 * KLON)
    attended, spectrum = pl.pallas_call(
        functools.partial(attend_kernel, len(others), first_row, sub),
        grid_spec=pltpu.PrefetchScalarGridSpec(
            num_scalar_prefetch=1,
            grid=(rows,),
            in_specs=[own_block] + [row_block] * len(others) + [whole(p) for p in params],
            out_specs=[row_block, spec_block],
            scratch_shapes=[pltpu.VMEM((points, feat), jnp.bfloat16)],
        ),
        out_shape=[
            jax.ShapeDtypeStruct((rows, points, feat), jnp.bfloat16),
            jax.ShapeDtypeStruct(spec_shape, jnp.bfloat16),
        ],
        cost_estimate=pl.CostEstimate(
            flops=flops, bytes_accessed=rows * points * feat * 8, transcendentals=rows * points * feat * 2
        ),
        compiler_params=pltpu.CompilerParams(vmem_limit_bytes=40 * 1024 * 1024),
        name=f"attend_{chunk}",
    )(counts, fields, *others, *params)
    if not aligned:
        spectrum = jnp.transpose(spectrum.reshape(rows, groups, held, feat), (1, 0, 2, 3))
    return attended, spectrum


def finish_kernel(first_row, counts, spectrum, attended, table, waves, *refs):
    out = refs[-1]
    feat = out.shape[-1]
    kept = waves[...] < counts[first_row + pl.program_id(0)]
    if len(spectrum.shape) == 4:
        spec = spectrum[:, 0].reshape(2 * KLON, feat)
    else:
        spec = spectrum[0]
    spec = jnp.where(kept, spec.astype(jnp.float32), 0.0).astype(jnp.bfloat16)
    out[0] = (attended[0].astype(jnp.float32) + dot(table[...], spec)).astype(jnp.bfloat16)


def finish(chunk, rows, lat_dev, aligned, groups, spectrum, attended, counts, table, waves, so_far):
    points, feat = attended.shape[1:]
    first_row = chunk * rows
    held = 2 * KLON // groups
    whole = lambda a: pl.BlockSpec(a.shape, lambda i, c: (0,) * a.ndim)
    if aligned:
        spec_block = pl.BlockSpec((groups, 1, held, feat), lambda i, c: (0, i, 0, 0))
    else:
        spectrum = jnp.transpose(spectrum, (1, 0, 2, 3)).reshape(rows, 2 * KLON, feat)
        spec_block = pl.BlockSpec((1, 2 * KLON, feat), lambda i, c: (i, 0, 0))
    row_block = pl.BlockSpec((1, points, feat), lambda i, c: (i, 0, 0))
    out_block = pl.BlockSpec((1, points, feat), lambda i, c: (first_row + i, 0, 0))
    operands = [counts, spectrum, attended, table, waves]
    specs = [spec_block, row_block, whole(table), whole(waves)]
    aliases = {}
    if so_far is not None:
        aliases = {len(operands): 0}
        operands.append(so_far)
        specs.append(pl.BlockSpec(memory_space=pl.ANY))
    return pl.pallas_call(
        functools.partial(finish_kernel, first_row),
        grid_spec=pltpu.PrefetchScalarGridSpec(
            num_scalar_prefetch=1, grid=(rows,), in_specs=specs, out_specs=out_block
        ),
        out_shape=jax.ShapeDtypeStruct((lat_dev, points, feat), jnp.bfloat16),
        input_output_aliases=aliases,
        cost_estimate=pl.CostEstimate(
            flops=4 * rows * points * feat * KLON,
            bytes_accessed=rows * points * feat * 6,
            transcendentals=0,
        ),
        compiler_params=pltpu.CompilerParams(vmem_limit_bytes=40 * 1024 * 1024),
        name=f"finish_{chunk}",
    )(*operands)


def shards(
    mesh_sizes, fields, mode_counts, gain_attn, w_query, w_key, w_value, w_out, gain_spec, w_first, w_second
):
    members, groups = mesh_sizes
    fields = fields[0]
    lat_dev, points, feat = fields.shape
    held = KLON // groups
    aligned = (2 * held) % 16 == 0
    chunks = max(c for c in range(1, CHUNKS + 1) if lat_dev % c == 0)
    rows = lat_dev // chunks
    shifts = [
        [(i, (i + s) % members) for i in range(members)] for s in range(1, members)
    ]
    others = [
        [lax.ppermute(fields[c * rows : (c + 1) * rows], "ens", s) for s in shifts]
        for c in range(chunks)
    ]
    w_qkv = jnp.concatenate([w_query, w_key, w_value], axis=1)
    lanes = jnp.arange(feat, dtype=jnp.int32) // HEAD
    sums = (lanes[:, None] == lanes[None, :]).astype(jnp.bfloat16)
    waves = wave_order(groups)[1][:, None]
    gains = (gain_attn[None, :], gain_spec[None, :])
    tables = (lon_forward(points, groups), sums, waves)
    back_table = lon_inverse(points, groups)
    forward = lat_forward(NLAT, KLAT).reshape(2, KLAT, 2, groups, chunks, rows)
    inverse = lat_inverse(NLAT, KLAT).reshape(2, 2, groups, chunks, rows, KLAT)
    big_one = complex_blocks(w_first)
    big_two = complex_blocks(w_second)
    kept_fields = []
    rows_spec = None
    for c in range(chunks):
        attended, spectrum = attend(
            c, rows, aligned, groups, fields, others[c], mode_counts, gains, (w_qkv, w_out), tables
        )
        kept_fields.append(attended)
        arrived = lax.all_to_all(spectrum, "grid", split_axis=0, concat_axis=0)
        arrived = arrived.reshape(groups, rows, 2, held, feat)
        term = jnp.einsum(
            "pqrgj,gjrkd->pqkd",
            forward[:, :, :, :, c],
            arrived,
            preferred_element_type=jnp.float32,
        )
        rows_spec = term if rows_spec is None else rows_spec + term
    rows_spec = rows_spec.astype(jnp.bfloat16)
    hidden = jnp.maximum(mix_blocks(rows_spec, big_one), 0.0).astype(jnp.bfloat16)
    second = mix_blocks(hidden, big_two).astype(jnp.bfloat16)
    out = None
    for c in range(chunks):
        back_rows = jnp.einsum(
            "rpgjq,pqkd->gjrkd", inverse[:, :, :, c], second, preferred_element_type=jnp.float32
        ).astype(jnp.bfloat16)
        returned = lax.all_to_all(
            back_rows.reshape(groups, rows, 2 * held, feat), "grid", split_axis=0, concat_axis=0
        )
        out = finish(
            c, rows, lat_dev, aligned, groups, returned, kept_fields[c], mode_counts, back_table,
            tables[2], out,
        )
    return out[None]


def solution(mesh):
    in_specs = (P("ens", "grid", None, None), P("grid"), P(), P(), P(), P(), P(), P(), P(), P())
    out_specs = P("ens", "grid", None, None)
    sizes = (mesh.shape["ens"], mesh.shape["grid"])
    return jax.shard_map(
        functools.partial(shards, sizes),
        mesh=mesh,
        in_specs=in_specs,
        out_specs=out_specs,
        check_vma=False,
    )
```

```python
import functools
import math

import jax
import jax.numpy as jnp
from jax import lax
from jax.experimental import pallas as pl
from jax.experimental.pallas import tpu as pltpu
from jax.sharding import PartitionSpec as P

HEAD = 32
NLAT = 384
KLON = 384
KLAT = 128
CHUNKS = 6
BACK_CHUNKS = 2

norm_eps = 1e-05


def layer_norm(widened, gain_vec):
    center = widened - jnp.mean(widened, axis=-1, keepdims=True)
    spread = jnp.mean(center * center, axis=-1, keepdims=True)
    return (center * lax.rsqrt(spread + norm_eps) * gain_vec).astype(jnp.bfloat16)


def wave_order(groups):
    held = KLON // groups
    place = jnp.arange(2 * KLON, dtype=jnp.int32)
    part = place // held % 2
    wave = place // (2 * held) * held + place % held
    return part, wave


def lon_forward(points, groups):
    part, wave = wave_order(groups)
    positions = jnp.arange(points, dtype=jnp.int32)
    turn_count = wave[:, None] * positions[None, :] % points
    angles = 2.0 * math.pi / points * turn_count.astype(jnp.float32)
    factor = 1.0 / math.sqrt(points)
    return jnp.where(
        part[:, None] == 0, jnp.cos(angles) * factor, -jnp.sin(angles) * factor
    ).astype(jnp.bfloat16)


def lon_inverse(points, groups):
    part, wave = wave_order(groups)
    positions = jnp.arange(points, dtype=jnp.int32)
    turn_count = positions[:, None] * wave[None, :] % points
    angles = 2.0 * math.pi / points * turn_count.astype(jnp.float32)
    weight = jnp.where(wave == 0, 1.0, 2.0).astype(jnp.float32)[None, :] / math.sqrt(points)
    return jnp.where(
        part[None, :] == 0, jnp.cos(angles) * weight, -jnp.sin(angles) * weight
    ).astype(jnp.bfloat16)


def lat_angles(row_count, mode_count):
    frequency = jnp.arange(mode_count, dtype=jnp.int32)
    frequency = jnp.where(frequency < mode_count // 2, frequency, frequency - mode_count)
    positions = jnp.arange(row_count, dtype=jnp.int32)
    turn_count = frequency[:, None] * positions[None, :] % row_count
    return 2.0 * math.pi / row_count * turn_count.astype(jnp.float32)


def lat_forward(row_count, mode_count):
    angles = lat_angles(row_count, mode_count)
    factor = 1.0 / math.sqrt(row_count)
    cosine = jnp.cos(angles) * factor
    sine_part = jnp.sin(angles) * factor
    return jnp.stack(
        [jnp.stack([cosine, sine_part], axis=1), jnp.stack([-sine_part, cosine], axis=1)]
    ).astype(jnp.bfloat16)


def lat_inverse(row_count, mode_count):
    angles = jnp.transpose(lat_angles(row_count, mode_count))
    factor = 1.0 / math.sqrt(row_count)
    cosine = jnp.cos(angles) * factor
    sine_part = jnp.sin(angles) * factor
    return jnp.stack([jnp.stack([cosine, -sine_part]), jnp.stack([sine_part, cosine])]).astype(
        jnp.bfloat16
    )


def complex_blocks(weight):
    real_part = weight[0]
    imag_part = weight[1]
    return jnp.stack([jnp.stack([real_part, imag_part]), jnp.stack([-imag_part, real_part])])


def mix_blocks(spec, big):
    blocks = spec.reshape(spec.shape[:3] + (big.shape[2], big.shape[3]))
    out_blocks = jnp.einsum("pqkbi,psbio->sqkbo", blocks, big, preferred_element_type=jnp.float32)
    return out_blocks.reshape(spec.shape)


def dot(left, right):
    return jnp.dot(left, right, preferred_element_type=jnp.float32)


def attend_kernel(others, first_row, sub, counts, own, *refs):
    other_refs = refs[:others]
    (gain_one, w_qkv, w_out, gain_two, table, sums, waves, attended, spectrum, normed) = refs[others:]
    points, feat = own.shape[1:]
    scale = 1.0 / math.sqrt(HEAD)
    for start in range(0, points, sub):
        rows = pl.ds(start, sub)
        fields = own[0, rows, :].astype(jnp.float32)
        joined = dot(layer_norm(fields, gain_one[...]), w_qkv[...]).astype(jnp.bfloat16)
        queries = joined[:, :feat].astype(jnp.float32)
        own_keys = joined[:, feat : 2 * feat].astype(jnp.float32)
        values = [joined[:, 2 * feat :].astype(jnp.float32)]
        shifted = [jnp.zeros((sub, feat), jnp.float32)]
        for ref in other_refs:
            side = layer_norm(ref[0, rows, :].astype(jnp.float32), gain_one[...])
            pair = dot(side, w_qkv[:, feat:]).astype(jnp.bfloat16)
            terms = queries * (pair[:, :feat].astype(jnp.float32) - own_keys)
            upper = terms.astype(jnp.bfloat16)
            lower = (terms - upper.astype(jnp.float32)).astype(jnp.bfloat16)
            total = dot(upper, sums[...]) + dot(lower, sums[...])
            shifted.append(total * scale)
            values.append(pair[:, feat:].astype(jnp.float32))
        largest = functools.reduce(jnp.maximum, shifted)
        exps = [jnp.exp(item - largest) for item in shifted]
        totals = functools.reduce(jnp.add, exps)
        mixed = functools.reduce(
            jnp.add,
            [e.astype(jnp.bfloat16).astype(jnp.float32) * v for e, v in zip(exps, values)],
        )
        mixed = (mixed / totals).astype(jnp.bfloat16)
        result = (fields + dot(mixed, w_out[...])).astype(jnp.bfloat16)
        attended[0, rows, :] = result
        normed[rows, :] = layer_norm(result.astype(jnp.float32), gain_two[...])
    kept = waves[...] < counts[first_row + pl.program_id(0)]
    spec = dot(table[...], normed[...])
    spec = jnp.where(kept, spec, 0.0).astype(jnp.bfloat16)
    if len(spectrum.shape) == 4:
        spectrum[:, 0] = spec.reshape(spectrum.shape[0], spectrum.shape[2], feat)
    else:
        spectrum[0] = spec


def attend(chunk, rows, aligned, groups, fields, others, counts, gains, weights, tables):
    points, feat = fields.shape[1:]
    first_row = chunk * rows
    sub = points // 3 if points % 48 == 0 else points
    whole = lambda a: pl.BlockSpec(a.shape, lambda i, c: (0,) * a.ndim)
    w_qkv, w_out = weights
    table, sums, waves = tables
    held = 2 * KLON // groups
    if aligned:
        spec_shape = (groups, rows, held, feat)
        spec_block = pl.BlockSpec((groups, 1, held, feat), lambda i, c: (0, i, 0, 0))
    else:
        spec_shape = (rows, 2 * KLON, feat)
        spec_block = pl.BlockSpec((1, 2 * KLON, feat), lambda i, c: (i, 0, 0))
    row_block = pl.BlockSpec((1, points, feat), lambda i, c: (i, 0, 0))
    own_block = pl.BlockSpec((1, points, feat), lambda i, c: (first_row + i, 0, 0))
    params = (gains[0], w_qkv, w_out, gains[1], table, sums, waves)
    flops = 2 * rows * points * feat * (feat * 8 + 2 * KLON)
    attended, spectrum = pl.pallas_call(
        functools.partial(attend_kernel, len(others), first_row, sub),
        grid_spec=pltpu.PrefetchScalarGridSpec(
            num_scalar_prefetch=1,
            grid=(rows,),
            in_specs=[own_block] + [row_block] * len(others) + [whole(p) for p in params],
            out_specs=[row_block, spec_block],
            scratch_shapes=[pltpu.VMEM((points, feat), jnp.bfloat16)],
        ),
        out_shape=[
            jax.ShapeDtypeStruct((rows, points, feat), jnp.bfloat16),
            jax.ShapeDtypeStruct(spec_shape, jnp.bfloat16),
        ],
        cost_estimate=pl.CostEstimate(
            flops=flops, bytes_accessed=rows * points * feat * 8, transcendentals=rows * points * feat * 2
        ),
        compiler_params=pltpu.CompilerParams(vmem_limit_bytes=40 * 1024 * 1024),
    )(counts, fields, *others, *params)
    if not aligned:
        spectrum = jnp.transpose(spectrum.reshape(rows, groups, held, feat), (1, 0, 2, 3))
    return attended, spectrum


def finish_kernel(first_row, counts, spectrum, attended, table, waves, *refs):
    out = refs[-1]
    feat = out.shape[-1]
    kept = waves[...] < counts[first_row + pl.program_id(0)]
    if len(spectrum.shape) == 4:
        spec = spectrum[:, 0].reshape(2 * KLON, feat)
    else:
        spec = spectrum[0]
    spec = jnp.where(kept, spec.astype(jnp.float32), 0.0).astype(jnp.bfloat16)
    out[0] = (attended[0].astype(jnp.float32) + dot(table[...], spec)).astype(jnp.bfloat16)


def finish(first_row, offset, lat_dev, aligned, groups, spectrum, attended, counts, table, waves, so_far):
    rows, points, feat = attended.shape
    held = 2 * KLON // groups
    whole = lambda a: pl.BlockSpec(a.shape, lambda i, c: (0,) * a.ndim)
    if aligned:
        spec_block = pl.BlockSpec((groups, 1, held, feat), lambda i, c: (0, offset + i, 0, 0))
    else:
        spectrum = jnp.transpose(spectrum, (1, 0, 2, 3)).reshape(-1, 2 * KLON, feat)
        spec_block = pl.BlockSpec((1, 2 * KLON, feat), lambda i, c: (offset + i, 0, 0))
    row_block = pl.BlockSpec((1, points, feat), lambda i, c: (i, 0, 0))
    out_block = pl.BlockSpec((1, points, feat), lambda i, c: (first_row + i, 0, 0))
    operands = [counts, spectrum, attended, table, waves]
    specs = [spec_block, row_block, whole(table), whole(waves)]
    aliases = {}
    if so_far is not None:
        aliases = {len(operands): 0}
        operands.append(so_far)
        specs.append(pl.BlockSpec(memory_space=pl.ANY))
    return pl.pallas_call(
        functools.partial(finish_kernel, first_row),
        grid_spec=pltpu.PrefetchScalarGridSpec(
            num_scalar_prefetch=1, grid=(rows,), in_specs=specs, out_specs=out_block
        ),
        out_shape=jax.ShapeDtypeStruct((lat_dev, points, feat), jnp.bfloat16),
        input_output_aliases=aliases,
        cost_estimate=pl.CostEstimate(
            flops=4 * rows * points * feat * KLON,
            bytes_accessed=rows * points * feat * 6,
            transcendentals=0,
        ),
        compiler_params=pltpu.CompilerParams(vmem_limit_bytes=40 * 1024 * 1024),
    )(*operands)


def shards(
    mesh_sizes, fields, mode_counts, gain_attn, w_query, w_key, w_value, w_out, gain_spec, w_first, w_second
):
    members, groups = mesh_sizes
    fields = fields[0]
    lat_dev, points, feat = fields.shape
    held = KLON // groups
    aligned = (2 * held) % 16 == 0
    chunks = max(c for c in range(1, CHUNKS + 1) if lat_dev % c == 0)
    rows = lat_dev // chunks
    shifts = [
        [(i, (i + s) % members) for i in range(members)] for s in range(1, members)
    ]
    others = []
    for c in range(chunks):
        others.append([lax.ppermute(fields[c * rows : (c + 1) * rows], "ens", s) for s in shifts])
    w_qkv = jnp.concatenate([w_query, w_key, w_value], axis=1)
    lanes = jnp.arange(feat, dtype=jnp.int32) // HEAD
    sums = (lanes[:, None] == lanes[None, :]).astype(jnp.bfloat16)
    waves = wave_order(groups)[1][:, None]
    gains = (gain_attn[None, :], gain_spec[None, :])
    tables = (lon_forward(points, groups), sums, waves)
    back_table = lon_inverse(points, groups)
    forward = lat_forward(NLAT, KLAT).reshape(2, KLAT, 2, groups, chunks, rows)
    backs = max(c for c in range(1, BACK_CHUNKS + 1) if chunks % c == 0)
    per_back = chunks // backs
    inverse = lat_inverse(NLAT, KLAT).reshape(2, 2, groups, backs, per_back * rows, KLAT)
    big_one = complex_blocks(w_first)
    big_two = complex_blocks(w_second)
    kept_fields = []
    rows_spec = None
    for c in range(chunks):
        attended, spectrum = attend(
            c, rows, aligned, groups, fields, others[c], mode_counts, gains, (w_qkv, w_out), tables
        )
        kept_fields.append(attended)
        arrived = lax.all_to_all(spectrum, "grid", split_axis=0, concat_axis=0)
        arrived = arrived.reshape(groups, rows, 2, held, feat)
        term = jnp.einsum(
            "pqrgj,gjrkd->pqkd",
            forward[:, :, :, :, c],
            arrived,
            preferred_element_type=jnp.float32,
        )
        rows_spec = term if rows_spec is None else rows_spec + term
        if c < chunks - 1:
            rows_spec = lax.optimization_barrier(rows_spec)
    rows_spec = rows_spec.astype(jnp.bfloat16)
    hidden = jnp.maximum(mix_blocks(rows_spec, big_one), 0.0).astype(jnp.bfloat16)
    second = mix_blocks(hidden, big_two).astype(jnp.bfloat16)
    out = None
    for b in range(backs):
        back_rows = jnp.einsum(
            "rpgjq,pqkd->gjrkd", inverse[:, :, :, b], second, preferred_element_type=jnp.float32
        ).astype(jnp.bfloat16)
        returned = lax.all_to_all(
            back_rows.reshape(groups, per_back * rows, 2 * held, feat), "grid", split_axis=0, concat_axis=0
        )
        for i in range(per_back):
            c = b * per_back + i
            out = finish(
                c * rows, i * rows, lat_dev, aligned, groups, returned, kept_fields[c], mode_counts,
                back_table, tables[2], out,
            )
    return out[None]


def layer(mesh_sizes, *args):
    return shards(mesh_sizes, *args)


def solution(mesh):
    in_specs = (P("ens", "grid", None, None), P("grid"), P(), P(), P(), P(), P(), P(), P(), P())
    out_specs = P("ens", "grid", None, None)
    sizes = (mesh.shape["ens"], mesh.shape["grid"])
    return jax.shard_map(
        functools.partial(layer, sizes),
        mesh=mesh,
        in_specs=in_specs,
        out_specs=out_specs,
        check_vma=False,
    )
```
